32 devices in a mesh: dp: 16 (over z, y, x), mp: 2 (over core).
Axes of the slice: x: 2, y: 2, z: 4, core: 2. Of those that a mesh axis runs over, the one named last changes fastest.
Arguments:
- query: bfloat16 [1024, 4096], P('dp', 'mp'), may hold values from -144 to 144
- new_key: bfloat16 [1024, 4096], P('dp', 'mp'), may hold values from -6 to 6
- new_value: bfloat16 [1024, 4096], P('dp', 'mp'), may hold values from -6 to 6
- cache_key: bfloat16 [1024, 32, 16, 128], P('dp', 'mp'), may hold values from -6 to 6
- cache_value: bfloat16 [1024, 32, 16, 128], P('dp', 'mp'), may hold values from -6 to 6
- cache_len: int32 [1024], P('dp'), may hold values from 2 to 16
- residual: bfloat16 [1024, 8192], P('dp'), may hold values from -6 to 6
- out_weight: bfloat16 [4096, 8192], P('mp'), may hold values from -0.1875 to 0.1875
- norm_gain: bfloat16 [8192], P('mp'), may hold values from 0.25 to 1.75
- codec_weight: bfloat16 [8192, 1024], P('mp'), may hold values from -0.125 to 0.125
- finished: int32 [1024], P('dp'), may hold values from 0 to 1
- owner: int32 [1024], P('dp'), may hold values from 0 to 15, as said below
- frames: bfloat16 [16384, 1024], P('dp', 'mp'), may hold values from -6 to 6
- snake_alpha: float32 [1024], P('mp'), may hold values from 0.5 to 2
- filter_weight: bfloat16 [7, 1024, 1024], P(None, None, 'mp'), may hold values from -0.125 to 0.125
- conv_bias: float32 [1024], P('mp'), may hold values from -4 to 4
Outputs:
- hidden: bfloat16 [1024, 8192], P('dp', 'mp')
- audio: bfloat16 [16384, 1024], P('dp', 'mp')
The draws below stay inside these ranges and needn't reach their ends.
Inputs may be any that keep to these rules, and one draw needn't show every extreme that they name: Within each aligned block of 64 rows, at most 4 finished rows name the same owner, and some owner is named by exactly 4 finished rows of the block.
All inputs are finite; a program needn't handle non-finite values.
Results may differ from the reference program's by a relative error of at most 0.0056.
Values may be sent and summed in bfloat16 or wider, within the bound.
A program may use at most 128 MiB of HBM per device.

```python
import math
import jax
import jax.numpy as jnp
from jax import lax

D = 8192
HEADS = 32
HD = 128
CODEC = 1024
ROW_DEV = 64
CACHE = 16
FRAMES = 1024
KERNEL_TAPS = 7
DILATION_STEP = 3
CAP = 4
ROWS = 1024
TOTAL_FRAMES = 16384
N_DP = 16


def key_tables(key):
    base = jax.random.fold_in(key, 11)
    first, second = jax.random.split(base, 2)
    keys = jnp.clip(jax.random.normal(first, (ROWS, HEADS, CACHE, HD), jnp.float32), -6.0, 6.0)
    queries = jnp.clip(jax.random.normal(second, (ROWS, HEADS, HD), jnp.float32), -6.0, 6.0)
    return (keys, queries.reshape(ROWS, HEADS * HD))


def draw_query(key, part):
    return key_tables(key)[1].astype(jnp.bfloat16)


def draw_cache_key(key, part):
    return key_tables(key)[0].astype(jnp.bfloat16)


def route_tables(key):
    base = jax.random.fold_in(key, 23)
    first, second, third = jax.random.split(base, 3)
    owners_perm = jax.vmap(lambda sub: jax.random.permutation(sub, N_DP))(jax.random.split(first, N_DP))
    orders = jax.vmap(lambda sub: jax.random.permutation(sub, ROW_DEV))(jax.random.split(second, N_DP))
    owners = jnp.take_along_axis(owners_perm, orders // CAP, axis=1)
    coins = (jax.random.randint(third, (N_DP, ROW_DEV), 0, 8) < 7).astype(jnp.int32)
    done = jnp.where(orders < CAP, 1, coins)
    return (owners.reshape(ROWS).astype(jnp.int32), done.reshape(ROWS).astype(jnp.int32))


def draw_owner(key, part):
    return route_tables(key)[0]


def draw_finished(key, part):
    return route_tables(key)[1]


def touch_ends(array, stream_key, smallest, top_value):
    dims = array.shape
    spot = [jax.random.randint(jax.random.fold_in(stream_key, axis), (), 0, dims[axis]) for axis in range(len(dims))]
    array = array.at[tuple(spot)].set(smallest)
    longest = dims.index(max(dims))
    spot[longest] = (spot[longest] + 1) % dims[longest]
    return array.at[tuple(spot)].set(top_value)


def steps_of(rng, dims, shards, smallest, high):
    factor_of, own = 1.0, jax.random.fold_in(rng, 6)
    for dim, shards_of in shards:
        heights = jnp.exp(jax.random.uniform(jax.random.fold_in(own, dim), (shards_of,), jnp.float32, smallest / len(shards), high / len(shards)))
        factor_of = factor_of * jnp.repeat(heights, dims[dim] // shards_of).reshape([-1 if axis == dim else 1 for axis in range(len(dims))])
    return factor_of


def noise(own_key, shape, width, reach, cuts=(), held_as=jnp.bfloat16):
    loudness = steps_of(own_key, shape, cuts, -0.22, 0.18) if cuts else 1.0
    result = jax.random.normal(own_key, shape, jnp.float32) * width * loudness
    return jnp.minimum(jnp.maximum(result, -reach), reach).astype(held_as)


def setup_inputs(seed: int = 0) -> dict:
    arg_keys = jax.random.split(jax.random.key(seed), 17)
    query = draw_query(jax.random.fold_in(arg_keys[16], 71), 0)
    new_key = noise(arg_keys[1], (ROWS, HEADS * HD), 1.0, 6.0, ((0, 16), (1, 2)))
    new_value = noise(arg_keys[2], (ROWS, HEADS * HD), 1.0, 6.0, ((0, 16), (1, 2)))
    cache_key = draw_cache_key(jax.random.fold_in(arg_keys[16], 71), 0)
    cache_value = noise(arg_keys[4], (ROWS, HEADS, CACHE, HD), 1.0, 6.0, ((0, 16), (1, 2)))
    cache_len = touch_ends(jax.random.randint(arg_keys[5], (ROWS,), 2, CACHE + 1), jax.random.fold_in(arg_keys[5], 1), 2, CACHE).astype(jnp.int32)
    residual = noise(arg_keys[6], (ROWS, D), 1.0, 6.0, ((0, 16),))
    out_weight = noise(arg_keys[7], (HEADS * HD, D), (HEADS * HD // 4) ** -0.5, 0.1875, ((0, 2),))
    norm_gain = jnp.clip(1.0 + 0.15 * jax.random.normal(arg_keys[8], (D,), jnp.float32), 0.25, 1.75).astype(jnp.bfloat16)
    codec_weight = noise(arg_keys[9], (D, CODEC), (D // 4) ** -0.5, 0.125, ((0, 2),))
    finished = draw_finished(jax.random.fold_in(arg_keys[16], 71), 0)
    owner = draw_owner(jax.random.fold_in(arg_keys[16], 71), 0)
    frames = noise(arg_keys[12], (TOTAL_FRAMES, CODEC), 1.0, 6.0, ((0, 16), (1, 2)))
    snake_alpha = jnp.clip(jnp.exp(math.log(2.0) - 1.3862944 * jax.random.uniform(arg_keys[13], (CODEC,), jnp.float32) ** steps_of(arg_keys[13], (CODEC,), ((0, 2),), -0.2, 0.2)), 0.5, 2.0)
    filter_weight = noise(arg_keys[14], (KERNEL_TAPS, CODEC, CODEC), (KERNEL_TAPS * CODEC // 4) ** -0.5, 0.125, ((2, 2),))
    conv_bias = noise(arg_keys[15], (CODEC,), 1.0, 4.0, ((0, 2),), jnp.float32)
    return dict(query=query, new_key=new_key, new_value=new_value, cache_key=cache_key, cache_value=cache_value, cache_len=cache_len, residual=residual, out_weight=out_weight, norm_gain=norm_gain, codec_weight=codec_weight, finished=finished, owner=owner, frames=frames, snake_alpha=snake_alpha, filter_weight=filter_weight, conv_bias=conv_bias)


def reference(query, new_key, new_value, cache_key, cache_value, cache_len, residual, out_weight, norm_gain, codec_weight, finished, owner, frames, snake_alpha, filter_weight, conv_bias):
    count = query.shape[0]
    heads = cache_key.shape[1]
    depth = cache_key.shape[3]
    positions = cache_key.shape[2]
    scale = 1.0 / jnp.sqrt(jnp.float32(depth))
    queries = query.reshape(count, heads, depth).astype(jnp.float32)
    fresh_key = new_key.reshape(count, heads, depth).astype(jnp.float32)
    fresh_value = new_value.reshape(count, heads, depth).astype(jnp.float32)
    scores = jnp.einsum('rhd,rhld->rhl', queries, cache_key.astype(jnp.float32)) * scale
    own_score = jnp.einsum('rhd,rhd->rh', queries, fresh_key) * scale
    valid = jnp.arange(positions, dtype=jnp.int32)[None, :] < cache_len[:, None]
    scores = jnp.where(valid[:, None, :], scores, -1e+30)
    top = jnp.maximum(lax.optimization_barrier(jnp.max(scores, axis=-1)), own_score)
    expo = jnp.where(valid[:, None, :], jnp.exp(scores - top[..., None]), 0.0)
    own_expo = jnp.exp(own_score - top)
    total = lax.optimization_barrier(jnp.sum(expo, axis=-1)) + own_expo
    weights = (expo / total[..., None]).astype(jnp.bfloat16)
    own_weight = (own_expo / total).astype(jnp.bfloat16)
    attended = jnp.einsum('rhl,rhld->rhd', weights.astype(jnp.float32), cache_value.astype(jnp.float32))
    attended = attended + own_weight.astype(jnp.float32)[..., None] * fresh_value
    attended = attended.astype(jnp.bfloat16).reshape(count, heads * depth)
    projected = jnp.dot(attended, out_weight, preferred_element_type=jnp.float32)
    hidden = (residual.astype(jnp.float32) + projected).astype(jnp.bfloat16)
    wide = hidden.astype(jnp.float32)
    meansq = lax.optimization_barrier(jnp.mean(wide * wide, axis=-1))
    normed = (wide * norm_gain.astype(jnp.float32)).astype(jnp.bfloat16)
    latent = jnp.dot(normed, codec_weight, preferred_element_type=jnp.float32) * lax.rsqrt(meansq + 1e-05)[:, None]
    latent = latent.astype(jnp.bfloat16)
    index = jnp.arange(count, dtype=jnp.int32)
    block = index // ROW_DEV
    earlier = (block[:, None] == block[None, :]) & (owner[:, None] == owner[None, :]) & (finished[None, :] == 1) & (index[None, :] < index[:, None])
    slot = lax.optimization_barrier(jnp.sum(earlier.astype(jnp.int32), axis=1)).astype(jnp.int32)
    overall_frames = frames.shape[0]
    target = (owner * FRAMES + block * CAP + slot).astype(jnp.int32)
    target = jnp.where(finished == 1, target, overall_frames).astype(jnp.int32)
    added = jnp.zeros(frames.shape, jnp.float32).at[target].add(latent.astype(jnp.float32), mode='drop')
    mix = frames.astype(jnp.float32) + added
    alpha = snake_alpha.astype(jnp.float32)
    act = (mix + jnp.sin(alpha * mix) ** 2 / alpha).astype(jnp.bfloat16)
    filter_span = KERNEL_TAPS // 2 * DILATION_STEP
    padded_frames = jnp.pad(act, ((filter_span, filter_span), (0, 0)))
    dilated_filter = jnp.zeros(mix.shape, jnp.float32)
    for tap_index in range(KERNEL_TAPS):
        dilated_filter = dilated_filter + jnp.dot(padded_frames[tap_index * DILATION_STEP:tap_index * DILATION_STEP + overall_frames], filter_weight[tap_index], preferred_element_type=jnp.float32)
    audio = (mix + conv_bias.astype(jnp.float32) + dilated_filter).astype(jnp.bfloat16)
    return (hidden, audio)
```

```python
import functools
import jax
import jax.numpy as jnp
from jax import lax
from jax.experimental import pallas as pl
from jax.experimental.pallas import tpu as pltpu
from jax.sharding import PartitionSpec as P

KERNEL_TAPS = 7
DILATION_STEP = 3
CAP = 4
ROW_TILE = 16


def swap(x):
    return lax.ppermute(x, "mp", [(0, 1), (1, 0)])


def gather_mp(x, axis):
    if lax.axis_size("mp") != 2:
        return lax.all_gather(x, "mp", axis=axis, tiled=True)
    other = swap(x)
    first = lax.axis_index("mp") == 0
    return jnp.concatenate([jnp.where(first, x, other), jnp.where(first, other, x)], axis=axis)


def sin_squared(x):
    turns = jnp.round(x * 0.3183098861837907)
    r = (x - turns * 3.140625) - turns * 0.0009676535897932
    q = r * r
    p = -2.5052108e-08 + q * 1.6059044e-10
    p = 2.7557319e-06 + q * p
    p = -1.9841270e-04 + q * p
    p = 8.3333333e-03 + q * p
    p = -1.6666667e-01 + q * p
    sine = r + r * (q * p)
    return sine * sine


def snake(mix, alpha):
    return (mix + sin_squared(alpha * mix) / alpha).astype(jnp.bfloat16)


def columns_kernel(start_ref, x_ref, w_ref, o_ref):
    del start_ref
    o_ref[...] = jnp.dot(x_ref[...], w_ref[...], preferred_element_type=jnp.float32).astype(
        o_ref.dtype
    )


def columns_dot(x, w, start, width, tile, dtype):
    rows, depth = x.shape
    return pl.pallas_call(
        columns_kernel,
        out_shape=jax.ShapeDtypeStruct((rows, width), dtype),
        grid_spec=pltpu.PrefetchScalarGridSpec(
            num_scalar_prefetch=1,
            grid=(width // tile,),
            in_specs=[
                pl.BlockSpec((rows, depth), lambda j, s: (0, 0)),
                pl.BlockSpec((depth, tile), lambda j, s: (0, s[0] + j)),
            ],
            out_specs=pl.BlockSpec((rows, tile), lambda j, s: (0, j)),
        ),
        compiler_params=pltpu.CompilerParams(vmem_limit_bytes=28 * 1024 * 1024),
        cost_estimate=pl.CostEstimate(
            flops=2 * rows * depth * width, bytes_accessed=2 * depth * width, transcendentals=0
        ),
    )(jnp.full((1,), start, jnp.int32), x, w)


def handoff_kernel(
    n_dp, n_mp, near, out_ref, a_ref, b_ref, land_a, land_b, send_a, recv_a, send_b, recv_b
):
    dp = lax.axis_index("dp")
    mp = lax.axis_index("mp")
    count = n_dp * n_mp
    me = dp * n_mp + mp
    barrier = pltpu.get_barrier_semaphore()

    def place(step):
        peer = lax.rem(me + step, count)
        return peer, peer // n_mp, lax.rem(peer, n_mp)

    def greet(step, carry):
        _, pd, pm = place(step)
        pl.semaphore_signal(
            barrier, inc=1, device_id=(pd, pm), device_id_type=pl.DeviceIdType.MESH
        )
        return carry

    lax.fori_loop(1, count, greet, 0)
    pl.semaphore_wait(barrier, count - 1)

    def copy_a(pd, pm, send, recv):
        return pltpu.make_async_remote_copy(
            src_ref=out_ref.at[pd],
            dst_ref=land_a.at[me],
            send_sem=send_a.at[send],
            recv_sem=recv_a.at[recv],
            device_id=(pd, pm),
            device_id_type=pl.DeviceIdType.MESH,
        )

    def copy_b(slot, pd, pm, send, recv):
        return pltpu.make_async_remote_copy(
            src_ref=out_ref.at[pd + 1],
            dst_ref=land_b.at[slot],
            send_sem=send_b.at[send],
            recv_sem=recv_b.at[recv],
            device_id=(pd, pm),
            device_id_type=pl.DeviceIdType.MESH,
        )

    def send(step, carry):
        peer, pd, pm = place(step)
        copy_a(pd, pm, peer, me).start()
        return carry

    def send_near(step, carry):
        peer, pd, pm = place(step)
        copy_b(me, pd, pm, peer, me).start()
        return carry

    @pl.when(dp < near)
    def _():
        lax.fori_loop(1, count, send_near, 0)

    lax.fori_loop(1, count, send, 0)
    land_a[me] = out_ref[dp]

    @pl.when(dp < near)
    def _():
        land_b[me] = out_ref[dp + 1]

    def finish(step, carry):
        peer, pd, pm = place(step)
        copy = copy_a(pd, pm, peer, peer)
        copy.wait_recv()
        copy.wait_send()
        return carry

    def finish_near(step, carry):
        peer, pd, pm = place(step)
        copy_b(me, pd, pm, peer, me).wait_send()
        return carry

    def take_near(sender, carry):
        @pl.when(sender != me)
        def _():
            copy_b(sender, 0, 0, sender, sender).wait_recv()

        return carry

    lax.fori_loop(1, count, finish, 0)

    @pl.when(dp < near)
    def _():
        lax.fori_loop(1, count, finish_near, 0)

    lax.fori_loop(0, near * n_mp, take_near, 0)

    def total_of(land, first):
        total = land[first].astype(jnp.float32)
        for m in range(1, n_mp):
            total = total + land[first + m].astype(jnp.float32)
        return total

    def put(d, carry):
        a_ref[d] = total_of(land_a, d * n_mp)
        return carry

    lax.fori_loop(0, n_dp, put, 0)
    for d in range(near):
        b_ref[d] = total_of(land_b, d * n_mp)


def handoff(outgoing, near):
    n_dp, n_mp = lax.axis_size("dp"), lax.axis_size("mp")
    count = n_dp * n_mp
    _, cap, width = outgoing.shape
    vmem = pl.BlockSpec(memory_space=pltpu.VMEM)
    return pl.pallas_call(
        functools.partial(handoff_kernel, n_dp, n_mp, near),
        out_shape=(
            jax.ShapeDtypeStruct((n_dp, cap, width), jnp.float32),
            jax.ShapeDtypeStruct((near, cap, width), jnp.float32),
        ),
        in_specs=[vmem],
        out_specs=(vmem, vmem),
        scratch_shapes=[
            pltpu.VMEM((count, cap, width), jnp.bfloat16),
            pltpu.VMEM((near * n_mp, cap, width), jnp.bfloat16),
            pltpu.SemaphoreType.DMA((count,)),
            pltpu.SemaphoreType.DMA((count,)),
            pltpu.SemaphoreType.DMA((count,)),
            pltpu.SemaphoreType.DMA((near * n_mp,)),
        ],
        compiler_params=pltpu.CompilerParams(
            collective_id=0, has_side_effects=True, vmem_limit_bytes=16 * 1024 * 1024
        ),
    )(outgoing)


def round_up(n, tile):
    return -(-n // tile) * tile


def taps_of(cells, rows):
    parts = [cells[t * DILATION_STEP : t * DILATION_STEP + rows] for t in range(KERNEL_TAPS)]
    return jnp.concatenate(parts, axis=1)


def attend(query, new_key, new_value, cache_key, cache_value, cache_len):
    count, heads, positions, depth = cache_key.shape
    scale = 1.0 / jnp.sqrt(jnp.float32(depth))
    queries = query.reshape(count, heads, depth)
    fresh_key = new_key.reshape(count, heads, depth)
    fresh_value = new_value.reshape(count, heads, depth)
    scores = (
        jnp.einsum("rhd,rhld->rhl", queries, cache_key, preferred_element_type=jnp.float32) * scale
    )
    own_score = (
        jnp.einsum("rhd,rhd->rh", queries, fresh_key, preferred_element_type=jnp.float32) * scale
    )
    valid = jnp.arange(positions, dtype=jnp.int32)[None, :] < cache_len[:, None]
    scores = jnp.where(valid[:, None, :], scores, -1e30)
    top = jnp.maximum(jnp.max(scores, axis=-1), own_score)
    expo = jnp.where(valid[:, None, :], jnp.exp(scores - top[..., None]), 0.0)
    own_expo = jnp.exp(own_score - top)
    total = jnp.sum(expo, axis=-1) + own_expo
    weights = (expo / total[..., None]).astype(jnp.bfloat16)
    own_weight = (own_expo / total).astype(jnp.bfloat16)
    mixed = jnp.einsum("rhl,rhld->rhd", weights, cache_value, preferred_element_type=jnp.float32)
    mixed = mixed + own_weight.astype(jnp.float32)[..., None] * fresh_value.astype(jnp.float32)
    return mixed.astype(jnp.bfloat16).reshape(count, heads * depth)


def body(
    query,
    new_key,
    new_value,
    cache_key,
    cache_value,
    cache_len,
    residual,
    out_weight,
    norm_gain,
    codec_weight,
    finished,
    owner,
    frames,
    snake_alpha,
    filter_weight,
    conv_bias,
):
    owners = lax.axis_size("dp")
    n_mp = lax.axis_size("mp")
    core = lax.axis_index("mp")
    tally, own = frames.shape
    span = KERNEL_TAPS // 2 * DILATION_STEP
    late = owners * CAP
    near = -(-span // CAP)
    front = round_up(late + span, ROW_TILE)
    back = round_up(span, ROW_TILE)

    wide_frames = frames.astype(jnp.float32)
    alpha_all = gather_mp(snake_alpha, 0)
    early = gather_mp(snake(wide_frames, snake_alpha), 1)
    head_frames = gather_mp(frames[:late], 1)
    before = lax.ppermute(early[tally - span :], "dp", [(i, i + 1) for i in range(owners - 1)])
    after_frames = lax.ppermute(
        head_frames[: near * CAP], "dp", [(i + 1, i) for i in range(owners - 1)]
    )
    middle = tally - front - back
    main = wide_frames[front : tally - back] + conv_bias
    for t in range(KERNEL_TAPS):
        start = front - span + t * DILATION_STEP
        main = main + jnp.dot(
            early[start : start + middle], filter_weight[t], preferred_element_type=jnp.float32
        )
    main = main.astype(jnp.bfloat16)

    attended = attend(query, new_key, new_value, cache_key, cache_value, cache_len)
    count = attended.shape[0]
    width = out_weight.shape[1]
    local_width = norm_gain.shape[0]
    residual_part = lax.dynamic_slice_in_dim(residual, core * local_width, local_width, 1)
    if n_mp == 2:
        tile = 1024
        theirs = columns_dot(
            attended, out_weight, (1 - core) * (local_width // tile), local_width, tile, jnp.bfloat16
        )
        arrived = swap(theirs)
        mine = columns_dot(
            attended, out_weight, core * (local_width // tile), local_width, tile, jnp.float32
        )
        projected = mine + arrived.astype(jnp.float32)
    else:
        term = jnp.dot(attended, out_weight, preferred_element_type=jnp.float32)
        projected = lax.psum_scatter(term, "mp", scatter_dimension=1, tiled=True)
    hidden = (residual_part.astype(jnp.float32) + projected).astype(jnp.bfloat16)
    wide = hidden.astype(jnp.float32)
    squares = jnp.sum(wide * wide, axis=-1)
    squares = squares + swap(squares) if n_mp == 2 else lax.psum(squares, "mp")
    meansq = squares / width
    normed = (wide * norm_gain.astype(jnp.float32)).astype(jnp.bfloat16)
    channels = codec_weight.shape[1]
    share = columns_dot(normed, codec_weight, 0, channels, 256, jnp.float32)
    share = (share * lax.rsqrt(meansq + 1e-05)[:, None]).astype(jnp.bfloat16)

    index = jnp.arange(count, dtype=jnp.int32)
    earlier = (
        (owner[:, None] == owner[None, :])
        & (finished[None, :] == 1)
        & (index[None, :] < index[:, None])
    )
    slot = jnp.sum(earlier.astype(jnp.int32), axis=1)
    target = owner * CAP + slot
    places = jnp.arange((owners + 1) * CAP, dtype=jnp.int32)
    onehot = ((places[:, None] == target[None, :]) & (finished[None, :] == 1)).astype(jnp.bfloat16)
    outgoing = jnp.dot(onehot, share, preferred_element_type=jnp.float32).astype(jnp.bfloat16)
    here, there = handoff(outgoing.reshape(owners + 1, CAP, channels), near)
    here = here.reshape(late, channels).astype(jnp.bfloat16).astype(jnp.float32)
    there = there.reshape(near * CAP, channels).astype(jnp.bfloat16).astype(jnp.float32)

    head_mix = head_frames.astype(jnp.float32) + here
    head_act = snake(head_mix, alpha_all)
    after = snake(after_frames.astype(jnp.float32) + there, alpha_all)[:span]
    cells_a = jnp.concatenate([before, head_act, early[late : front + span]], axis=0)
    cells_b = jnp.concatenate([early[tally - back - span :], after], axis=0)
    edges = jnp.concatenate([taps_of(cells_a, front), taps_of(cells_b, back)], axis=0)
    flat = filter_weight.reshape(KERNEL_TAPS * channels, own)
    own_mix = lax.dynamic_slice_in_dim(head_mix, core * own, own, 1)
    edge_mix = jnp.concatenate(
        [own_mix, wide_frames[late:front], wide_frames[tally - back :]], axis=0
    )
    edge = jnp.dot(edges, flat, preferred_element_type=jnp.float32) + edge_mix + conv_bias
    edge = edge.astype(jnp.bfloat16)
    audio = jnp.concatenate([edge[:front], main, edge[front:]], axis=0)
    return (hidden, audio)


def solution(mesh):
    placed = (
        P("dp", "mp"),
        P("dp", "mp"),
        P("dp", "mp"),
        P("dp", "mp", None, None),
        P("dp", "mp", None, None),
        P("dp"),
        P("dp", None),
        P("mp", None),
        P("mp"),
        P("mp", None),
        P("dp"),
        P("dp"),
        P("dp", "mp"),
        P("mp"),
        P(None, None, "mp"),
        P("mp"),
    )
    return jax.shard_map(
        body, mesh=mesh, in_specs=placed, out_specs=(P("dp", "mp"), P("dp", "mp")), check_vma=False
    )
```

```python
import functools
import jax
import jax.numpy as jnp
from jax import lax
from jax.experimental import pallas as pl
from jax.experimental.pallas import tpu as pltpu
from jax.sharding import PartitionSpec as P

KERNEL_TAPS = 7
DILATION_STEP = 3
CAP = 4
ROW_TILE = 16


def swap(x):
    return lax.ppermute(x, "mp", [(0, 1), (1, 0)])


def gather_mp(x, axis):
    if lax.axis_size("mp") != 2:
        return lax.all_gather(x, "mp", axis=axis, tiled=True)
    other = swap(x)
    first = lax.axis_index("mp") == 0
    return jnp.concatenate([jnp.where(first, x, other), jnp.where(first, other, x)], axis=axis)


def sin_squared(x):
    turns = jnp.round(x * 0.3183098861837907)
    r = (x - turns * 3.140625) - turns * 0.0009676535897932
    q = r * r
    p = -2.5052108e-08 + q * 1.6059044e-10
    p = 2.7557319e-06 + q * p
    p = -1.9841270e-04 + q * p
    p = 8.3333333e-03 + q * p
    p = -1.6666667e-01 + q * p
    sine = r + r * (q * p)
    return sine * sine


def snake(mix, alpha):
    return (mix + sin_squared(alpha * mix) * (1.0 / alpha)).astype(jnp.bfloat16)


def columns_kernel(start_ref, x_ref, w_ref, o_ref):
    del start_ref
    o_ref[...] = jnp.dot(x_ref[...], w_ref[...], preferred_element_type=jnp.float32).astype(
        o_ref.dtype
    )


def columns_dot(x, w, start, width, tile, dtype):
    rows, depth = x.shape
    return pl.pallas_call(
        columns_kernel,
        out_shape=jax.ShapeDtypeStruct((rows, width), dtype),
        grid_spec=pltpu.PrefetchScalarGridSpec(
            num_scalar_prefetch=1,
            grid=(width // tile,),
            in_specs=[
                pl.BlockSpec((rows, depth), lambda j, s: (0, 0)),
                pl.BlockSpec((depth, tile), lambda j, s: (0, s[0] + j)),
            ],
            out_specs=pl.BlockSpec((rows, tile), lambda j, s: (0, j)),
        ),
        compiler_params=pltpu.CompilerParams(vmem_limit_bytes=60 * 1024 * 1024),
        cost_estimate=pl.CostEstimate(
            flops=2 * rows * depth * width, bytes_accessed=2 * depth * width, transcendentals=0
        ),
    )(jnp.full((1,), start, jnp.int32), x, w)


def handoff_kernel(
    n_dp, n_mp, near, out_ref, a_ref, b_ref, land_a, land_b,
    own_sem, send_a, recv_a, send_b, recv_b, share_send, share_recv,
):
    dp = lax.axis_index("dp")
    mp = lax.axis_index("mp")
    barrier = pltpu.get_barrier_semaphore()
    mesh_id = pl.DeviceIdType.MESH
    width = out_ref.shape[2]

    def peer_of(step):
        return lax.rem(dp + step, n_dp)

    def core_of(step):
        return lax.rem(mp + step, n_mp)

    def greet(step, carry):
        pl.semaphore_signal(barrier, inc=1, device_id=(peer_of(step), mp), device_id_type=mesh_id)
        return carry

    lax.fori_loop(1, n_dp, greet, 0)
    for c in range(1, n_mp):
        pl.semaphore_signal(barrier, inc=1, device_id=(dp, core_of(c)), device_id_type=mesh_id)
    pl.semaphore_wait(barrier, n_dp - 1 + n_mp - 1)

    def copy_a(pd, recv):
        return pltpu.make_async_remote_copy(
            src_ref=out_ref.at[pd],
            dst_ref=land_a.at[mp, dp],
            send_sem=send_a.at[pd],
            recv_sem=recv_a.at[recv],
            device_id=(pd, mp),
            device_id_type=mesh_id,
        )

    def copy_b(slot, pd, recv):
        return pltpu.make_async_remote_copy(
            src_ref=out_ref.at[pd + 1],
            dst_ref=land_b.at[mp, slot],
            send_sem=send_b.at[pd],
            recv_sem=recv_b.at[recv],
            device_id=(pd, mp),
            device_id_type=mesh_id,
        )

    def share(ref, kind, c, core, slot):
        return pltpu.make_async_remote_copy(
            src_ref=ref.at[mp],
            dst_ref=ref.at[slot],
            send_sem=share_send.at[kind, c],
            recv_sem=share_recv.at[kind, c],
            device_id=(dp, core),
            device_id_type=mesh_id,
        )

    def send(step, carry):
        pd = peer_of(step)
        copy_a(pd, dp).start()
        return carry

    def send_near(step, carry):
        copy_b(dp, peer_of(step), dp).start()
        return carry

    lax.fori_loop(1, n_dp, send, 0)
    own_a = pltpu.make_async_copy(out_ref.at[dp], land_a.at[mp, dp], own_sem.at[0])
    own_a.start()

    @pl.when(dp < near)
    def _():
        lax.fori_loop(1, n_dp, send_near, 0)
        own_b = pltpu.make_async_copy(out_ref.at[dp + 1], land_b.at[mp, dp], own_sem.at[1])
        own_b.start()
        own_b.wait()

    own_a.wait()

    def finish(step, carry):
        pd = peer_of(step)
        copy_a(pd, pd).wait_recv()
        return carry

    def leave(step, carry):
        copy_a(peer_of(step), dp).wait_send()
        return carry

    def leave_near(step, carry):
        copy_b(dp, peer_of(step), dp).wait_send()
        return carry

    def take_near(sender, carry):
        @pl.when(sender != dp)
        def _():
            copy_b(sender, 0, sender).wait_recv()

        return carry

    lax.fori_loop(1, n_dp, finish, 0)
    for c in range(1, n_mp):
        share(land_a, 0, c, core_of(c), mp).start()
    lax.fori_loop(0, near, take_near, 0)
    for c in range(1, n_mp):
        share(land_b, 1, c, core_of(c), mp).start()
    lax.fori_loop(1, n_dp, leave, 0)

    @pl.when(dp < near)
    def _():
        lax.fori_loop(1, n_dp, leave_near, 0)

    for kind, ref in ((0, land_a), (1, land_b)):
        for c in range(1, n_mp):
            copy = share(ref, kind, c, core_of(c), core_of(n_mp - c))
            copy.wait_send()
            copy.wait_recv()
    for m in range(n_mp):
        a_ref[:, :, m * width : (m + 1) * width] = land_a[m].astype(jnp.float32)
        b_ref[:, :, m * width : (m + 1) * width] = land_b[m].astype(jnp.float32)


def handoff(outgoing, near):
    n_dp, n_mp = lax.axis_size("dp"), lax.axis_size("mp")
    _, cap, width = outgoing.shape
    vmem = pl.BlockSpec(memory_space=pltpu.VMEM)
    dma = pltpu.SemaphoreType.DMA
    return pl.pallas_call(
        functools.partial(handoff_kernel, n_dp, n_mp, near),
        out_shape=(
            jax.ShapeDtypeStruct((n_dp, cap, n_mp * width), jnp.float32),
            jax.ShapeDtypeStruct((near, cap, n_mp * width), jnp.float32),
        ),
        in_specs=[vmem],
        out_specs=(vmem, vmem),
        scratch_shapes=[
            pltpu.VMEM((n_mp, n_dp, cap, width), jnp.bfloat16),
            pltpu.VMEM((n_mp, near, cap, width), jnp.bfloat16),
            dma((2,)),
            dma((n_dp,)),
            dma((n_dp,)),
            dma((n_dp,)),
            dma((near,)),
            dma((2, n_mp)),
            dma((2, n_mp)),
        ],
        compiler_params=pltpu.CompilerParams(
            collective_id=0, has_side_effects=True, vmem_limit_bytes=16 * 1024 * 1024
        ),
    )(outgoing)


def round_up(n, tile):
    return -(-n // tile) * tile


def taps_of(cells, rows):
    parts = [cells[t * DILATION_STEP : t * DILATION_STEP + rows] for t in range(KERNEL_TAPS)]
    return jnp.concatenate(parts, axis=1)


def attend(query, new_key, new_value, cache_key, cache_value, cache_len):
    count, heads, positions, depth = cache_key.shape
    scale = 1.0 / jnp.sqrt(jnp.float32(depth))
    queries = query.reshape(count, heads, depth)
    fresh_key = new_key.reshape(count, heads, depth)
    fresh_value = new_value.reshape(count, heads, depth)
    scores = (
        jnp.einsum("rhd,rhld->rhl", queries, cache_key, preferred_element_type=jnp.float32) * scale
    )
    own_score = (
        jnp.einsum("rhd,rhd->rh", queries, fresh_key, preferred_element_type=jnp.float32) * scale
    )
    valid = jnp.arange(positions, dtype=jnp.int32)[None, :] < cache_len[:, None]
    scores = jnp.where(valid[:, None, :], scores, -1e30)
    top = jnp.maximum(jnp.max(scores, axis=-1), own_score)
    expo = jnp.where(valid[:, None, :], jnp.exp(scores - top[..., None]), 0.0)
    own_expo = jnp.exp(own_score - top)
    total = jnp.sum(expo, axis=-1) + own_expo
    weights = (expo / total[..., None]).astype(jnp.bfloat16)
    own_weight = (own_expo / total).astype(jnp.bfloat16)
    mixed = jnp.einsum("rhl,rhld->rhd", weights, cache_value, preferred_element_type=jnp.float32)
    mixed = mixed + own_weight.astype(jnp.float32)[..., None] * fresh_value.astype(jnp.float32)
    return mixed.astype(jnp.bfloat16).reshape(count, heads * depth)


def body(
    query,
    new_key,
    new_value,
    cache_key,
    cache_value,
    cache_len,
    residual,
    out_weight,
    norm_gain,
    codec_weight,
    finished,
    owner,
    frames,
    snake_alpha,
    filter_weight,
    conv_bias,
):
    owners = lax.axis_size("dp")
    n_mp = lax.axis_size("mp")
    core = lax.axis_index("mp")
    tally, own = frames.shape
    span = KERNEL_TAPS // 2 * DILATION_STEP
    late = owners * CAP
    near = -(-span // CAP)
    front = round_up(late + span, ROW_TILE)
    back = round_up(span, ROW_TILE)

    wide_frames = frames.astype(jnp.float32)
    alpha_all = gather_mp(snake_alpha, 0)
    early = gather_mp(snake(wide_frames, snake_alpha), 1)
    ends = gather_mp(jnp.concatenate([frames[:late], frames[tally - back :]], axis=0), 1)
    head_frames = ends[:late]
    before = lax.ppermute(ends[late:], "dp", [(i, i + 1) for i in range(owners - 1)])
    after_frames = lax.ppermute(
        head_frames[: near * CAP], "dp", [(i + 1, i) for i in range(owners - 1)]
    )
    middle = tally - front - back
    main = wide_frames[front : tally - back] + conv_bias
    for t in range(KERNEL_TAPS):
        start = front - span + t * DILATION_STEP
        main = main + jnp.dot(
            early[start : start + middle], filter_weight[t], preferred_element_type=jnp.float32
        )
    main = main.astype(jnp.bfloat16)

    attended = attend(query, new_key, new_value, cache_key, cache_value, cache_len)
    count = attended.shape[0]
    width = out_weight.shape[1]
    local_width = norm_gain.shape[0]
    residual_part = lax.dynamic_slice_in_dim(residual, core * local_width, local_width, 1)
    if n_mp == 2:
        tile = 1024
        theirs = columns_dot(
            attended, out_weight, (1 - core) * (local_width // tile), local_width, tile, jnp.bfloat16
        )
        arrived = swap(theirs)
        mine = columns_dot(
            attended, out_weight, core * (local_width // tile), local_width, tile, jnp.float32
        )
        projected = mine + arrived.astype(jnp.float32)
    else:
        term = jnp.dot(attended, out_weight, preferred_element_type=jnp.float32)
        projected = lax.psum_scatter(term, "mp", scatter_dimension=1, tiled=True)
    hidden = (residual_part.astype(jnp.float32) + projected).astype(jnp.bfloat16)
    wide = hidden.astype(jnp.float32)
    squares = jnp.sum(wide * wide, axis=-1)
    squares = squares + swap(squares) if n_mp == 2 else lax.psum(squares, "mp")
    meansq = squares / width
    normed = (wide * norm_gain.astype(jnp.float32)).astype(jnp.bfloat16)
    channels = codec_weight.shape[1]
    share = columns_dot(normed, codec_weight, 0, channels, 256, jnp.float32)
    if n_mp == 2:
        given = lax.dynamic_slice_in_dim(share, (1 - core) * own, own, 1).astype(jnp.bfloat16)
        kept = lax.dynamic_slice_in_dim(share, core * own, own, 1)
        latent = kept + swap(given).astype(jnp.float32)
    else:
        latent = lax.psum_scatter(share, "mp", scatter_dimension=1, tiled=True)
    latent = (latent * lax.rsqrt(meansq + 1e-05)[:, None]).astype(jnp.bfloat16)

    index = jnp.arange(count, dtype=jnp.int32)
    earlier = (
        (owner[:, None] == owner[None, :])
        & (finished[None, :] == 1)
        & (index[None, :] < index[:, None])
    )
    slot = jnp.sum(earlier.astype(jnp.int32), axis=1)
    target = owner * CAP + slot
    places = jnp.arange((owners + 1) * CAP, dtype=jnp.int32)
    onehot = ((places[:, None] == target[None, :]) & (finished[None, :] == 1)).astype(jnp.bfloat16)
    outgoing = jnp.dot(onehot, latent, preferred_element_type=jnp.float32).astype(jnp.bfloat16)
    here, there = handoff(outgoing.reshape(owners + 1, CAP, own), near)
    here = here.reshape(late, channels)
    there = there.reshape(near * CAP, channels)

    head_mix = head_frames.astype(jnp.float32) + here
    head_act = snake(head_mix, alpha_all)
    after = snake(after_frames.astype(jnp.float32) + there, alpha_all)[:span]
    before = snake(before.astype(jnp.float32), alpha_all)[back - span :]
    cells_a = jnp.concatenate([before, head_act, early[late : front + span]], axis=0)
    cells_b = jnp.concatenate([early[tally - back - span :], after], axis=0)
    edges = jnp.concatenate([taps_of(cells_a, front), taps_of(cells_b, back)], axis=0)
    flat = filter_weight.reshape(KERNEL_TAPS * channels, own)
    own_mix = lax.dynamic_slice_in_dim(head_mix, core * own, own, 1)
    edge_mix = jnp.concatenate(
        [own_mix, wide_frames[late:front], wide_frames[tally - back :]], axis=0
    )
    edge = jnp.dot(edges, flat, preferred_element_type=jnp.float32) + edge_mix + conv_bias
    edge = edge.astype(jnp.bfloat16)
    audio = jnp.concatenate([edge[:front], main, edge[front:]], axis=0)
    return (hidden, audio)


def solution(mesh):
    placed = (
        P("dp", "mp"),
        P("dp", "mp"),
        P("dp", "mp"),
        P("dp", "mp", None, None),
        P("dp", "mp", None, None),
        P("dp"),
        P("dp", None),
        P("mp", None),
        P("mp"),
        P("mp", None),
        P("dp"),
        P("dp"),
        P("dp", "mp"),
        P("mp"),
        P(None, None, "mp"),
        P("mp"),
    )
    return jax.shard_map(
        body, mesh=mesh, in_specs=placed, out_specs=(P("dp", "mp"), P("dp", "mp")), check_vma=False
    )
```
